32 devices in a mesh: trip: 4 (over x, core), exc: 8 (over z, y).
Axes of the slice: x: 2, y: 2, z: 4, core: 2. Of those that a mesh axis runs over, the one named last changes fastest.
Arguments:
- pes_grids: float32 [128, 16, 256], P(('trip', 'exc')), may hold values from -6 to 6
- modals: float32 [200, 128], P('trip'), may hold values from -1.8 to 1.8
- energies: float32 [200, 8], P('trip'), may hold values from 0.05 to 0.5
- triple_modes: int32 [128, 3], P(('trip', 'exc')), may hold values from 0 to 199, as said below
- routing: int32 [4, 8, 8], P('trip', None, 'exc'), may hold values from 0 to 3
- block_source: int32 [768], P(('trip', 'exc')), may hold values from 0 to 7
- live_rows: int32 [768], P(('trip', 'exc')), may hold values from 1 to 8
- trial_vectors: bfloat16 [768, 512, 512], P(('trip', 'exc')), may hold values from -6 to 6
- spectator_energy: float32 [768, 8], P(('trip', 'exc')), may hold values from 0.1 to 1
Outputs:
- sigma_blocks: bfloat16 [768, 512, 512], P(('trip', 'exc'))
The draws below stay inside these ranges and needn't reach their ends.
Inputs may be any that keep to these rules, and one draw needn't show every extreme that they name: `triple_modes`: the three modes of a triple are distinct.
All inputs are finite; a program needn't handle non-finite values.
Results may differ from the reference program's by a relative error of at most 0.005.
Values may be sent and summed in bfloat16 or wider, within the bound.
A program may use at most 128 MiB of HBM per device.

```python
import math
import jax
import jax.numpy as jnp
import numpy as np
from jax import lax

MODES = 200
NMOD = 8
G = 16
NVEC = 64
ROWS = 8
BLK_DEV = 24
TRI_DEV = 4
S = 512
SLABS = 4
COLS = 8
NTRI = 128
NBLK = 768


def draw_triple_modes(key, part):
    subkeys = jax.random.split(key, 3)
    mode_one = jax.random.randint(subkeys[0], (NTRI,), 0, MODES)
    step_one = jax.random.randint(subkeys[1], (NTRI,), 1, MODES // 2)
    step_two = jax.random.randint(subkeys[2], (NTRI,), 1, MODES // 2)
    mode_two = (mode_one + step_one) % MODES
    mode_three = (mode_two + step_two) % MODES
    return jnp.stack([mode_one, mode_two, mode_three], axis=1).astype(jnp.int32)


def draw_live_rows(key, part):
    subkeys = jax.random.split(key, 2)
    drawn = jax.random.randint(subkeys[0], (NBLK,), 1, ROWS + 1)
    chosen = jax.random.randint(subkeys[1], (), 0, NBLK)
    return drawn.at[chosen].set(ROWS).astype(jnp.int32)


def with_ends(entries, own_key, smallest, largest):
    spot = [jax.random.randint(jax.random.fold_in(own_key, axis), (), 0, length) for axis, length in enumerate(entries.shape)]
    main_axis = entries.shape.index(max(entries.shape))
    beside = spot[:main_axis] + [(spot[main_axis] + 1) % entries.shape[main_axis]] + spot[main_axis + 1:]
    return entries.at[tuple(spot)].set(smallest).at[tuple(beside)].set(largest)


def steps_of(key, extent, cuts, smallest, largest):
    gain, own = 1.0, jax.random.fold_in(key, 6)
    for position, shards_of in cuts:
        heights = jnp.exp(jax.random.uniform(jax.random.fold_in(own, position), (shards_of,), jnp.float32, smallest / len(cuts), largest / len(cuts)))
        gain = gain * jnp.repeat(heights, extent[position] // shards_of).reshape([-1 if axis == position else 1 for axis in range(len(extent))])
    return gain


def rank_bounds(number_of, slope):
    portions = [(1 << 20) // math.isqrt(grade ** slope) + 1 for grade in range(1, number_of + 1)]
    width = 1 + sum(portions) // (1 << 30)
    return np.cumsum(np.array([max(1, weight // width) for weight in portions]))


def ranked(own_key, dims, count, lean):
    grid = rank_bounds(count, lean)
    lot = jax.random.randint(jax.random.fold_in(own_key, 1), dims, 0, int(grid[count - 1]))
    grade = jnp.searchsorted(jnp.asarray(grid, jnp.int32), lot, side="right")
    return jax.random.permutation(jax.random.fold_in(own_key, 2), count)[grade].astype(jnp.int32)


def normal_values(rng, dims, scale, most, pieces=(), kind=jnp.bfloat16):
    result = jax.random.normal(rng, dims, jnp.float32) * scale
    if len(pieces) > 0:
        result = steps_of(rng, dims, pieces, -0.22, 0.18) * result
    return jnp.clip(result, min=-most, max=most).astype(kind)


def setup_inputs(seed: int = 0) -> dict:
    key_of = jax.random.split(jax.random.key(seed), 10)
    pes_grids = normal_values(key_of[0], (NTRI, G, G * G), 1.0, 6.0, ((0, 32),), jnp.float32)
    modals = normal_values(key_of[1], (MODES, NMOD * G), 0.3, 1.8, ((0, 4),), jnp.float32)
    energies = jnp.clip(jnp.exp(math.log(0.5) - 2.3025851 * jax.random.uniform(key_of[2], (MODES, NMOD), jnp.float32) ** steps_of(key_of[2], (MODES, NMOD), ((0, 4),), -0.2, 0.2)), 0.05, 0.5)
    triple_modes = draw_triple_modes(jax.random.fold_in(key_of[9], 71), 0)
    routing = with_ends(jax.random.randint(key_of[4], (SLABS, COLS, COLS), 0, TRI_DEV), jax.random.fold_in(key_of[4], 1), 0, TRI_DEV - 1).astype(jnp.int32)
    block_source = with_ends(ranked(key_of[5], (NBLK,), COLS, 2), jax.random.fold_in(key_of[5], 3), 0, COLS - 1).astype(jnp.int32)
    live_rows = draw_live_rows(jax.random.fold_in(key_of[9], 71), 0)
    trial_vectors = normal_values(key_of[7], (NBLK, S, ROWS * NVEC), 1.0, 6.0, ((0, 32),))
    spectator_energy = jnp.clip(jnp.exp(math.log(1.0) - 2.3025851 * jax.random.uniform(key_of[8], (NBLK, ROWS), jnp.float32) ** steps_of(key_of[8], (NBLK, ROWS), ((0, 32),), -0.2, 0.2)), 0.1, 1.0)
    return dict(pes_grids=pes_grids, modals=modals, energies=energies, triple_modes=triple_modes, routing=routing, block_source=block_source, live_rows=live_rows, trial_vectors=trial_vectors, spectator_energy=spectator_energy)


def integrals(grid_values, modal_rows, level_rows):
    shaped = modal_rows.reshape(3, NMOD, G)
    paired = (shaped[:, :, None, :] * shaped[:, None, :, :]).reshape(3, NMOD * NMOD, G)
    grid_cube = grid_values.reshape(G, G, G)
    section_one = jnp.einsum("xyz,cz->xyc", grid_cube, paired[2], precision=lax.Precision.HIGHEST)
    section_two = jnp.einsum("xyc,by->xbc", section_one, paired[1], precision=lax.Precision.HIGHEST)
    tensor = jnp.einsum("xbc,ax->abc", section_two, paired[0], precision=lax.Precision.HIGHEST)
    states = NMOD * NMOD * NMOD
    matrix = tensor.reshape(NMOD, NMOD, NMOD, NMOD, NMOD, NMOD).transpose(0, 2, 4, 1, 3, 5).reshape(states, states)
    diagonal = (level_rows[0][:, None, None] + level_rows[1][None, :, None] + level_rows[2][None, None, :]).reshape(states)
    return (matrix + jnp.diag(diagonal)).astype(jnp.bfloat16)


def apply_block(matrix, coeff_block, spec_row, live_count):
    product = jnp.dot(matrix, coeff_block, preferred_element_type=jnp.float32)
    spread = jnp.repeat(spec_row, NVEC)
    summed = product + spread[None, :] * coeff_block.astype(jnp.float32)
    column_rows = jnp.arange(ROWS * NVEC, dtype=jnp.int32) // NVEC
    return jnp.where((column_rows < live_count)[None, :], summed, 0.0).astype(jnp.bfloat16)


def reference(pes_grids, modals, energies, triple_modes, routing, block_source, live_rows, trial_vectors, spectator_energy):
    block_ids = jnp.arange(NBLK, dtype=jnp.int32)
    device = block_ids // BLK_DEV
    slab_of = device // COLS
    column = device % COLS
    local_id = routing[slab_of, column, block_source]
    triple_ids = ((slab_of * COLS + block_source) * TRI_DEV + local_id).astype(jnp.int32)

    def one_block(packed):
        triple_id, coeff_block, spec_row, live_count = packed
        mode_ids = triple_modes[triple_id]
        matrix = integrals(pes_grids[triple_id], modals[mode_ids], energies[mode_ids])
        return apply_block(matrix, coeff_block, spec_row, live_count)

    return lax.map(one_block, (triple_ids, trial_vectors, spectator_energy, live_rows))
```

```python
import functools

import jax
import jax.numpy as jnp
from jax import lax
from jax.experimental import pallas as pl
from jax.experimental.pallas import tpu as pltpu
from jax.sharding import PartitionSpec as P

NMOD = 8
G = 16
F32 = jnp.float32
BF16 = jnp.bfloat16
MESH = pl.DeviceIdType.MESH
LANES = 128


def exchange(
    n_trip,
    n_exc,
    routing_ref,
    modes_ref,
    grids_ref,
    modals_ref,
    energies_ref,
    table_ref,
    levels_ref,
    grid_out_ref,
    mode_out_ref,
    send_grid,
    send_mode,
    trip_send,
    trip_recv,
    exc_send,
    exc_recv,
):
    me_t = lax.axis_index("trip")
    me_e = lax.axis_index("exc")
    barrier = pltpu.get_barrier_semaphore()
    for step in range(1, n_exc):
        peer = lax.rem(me_e + step, n_exc)
        pl.semaphore_signal(barrier, inc=1, device_id={"exc": peer}, device_id_type=MESH)
    for step in range(1, n_trip):
        peer = lax.rem(me_t + step, n_trip)
        pl.semaphore_signal(barrier, inc=1, device_id={"trip": peer}, device_id_type=MESH)
    lane = lax.broadcasted_iota(jnp.int32, (1, LANES), 1)
    for column in range(n_exc):
        wanted = routing_ref[0, column, 0]
        send_grid[column] = grids_ref[wanted]
        send_mode[column] = jnp.where(
            lane == 0,
            modes_ref[wanted, 0],
            jnp.where(lane == 1, modes_ref[wanted, 1], modes_ref[wanted, 2]),
        )
    table_ref[me_t] = modals_ref[...]
    levels_ref[me_t] = energies_ref[...]
    grid_out_ref[me_e] = send_grid[me_e]
    mode_out_ref[me_e] = send_mode[me_e]
    pl.semaphore_wait(barrier, n_exc - 1 + n_trip - 1)

    def trip_copies(step, slot):
        peer = lax.rem(me_t + step, n_trip)
        for kind, (src, dst) in enumerate(((modals_ref, table_ref), (energies_ref, levels_ref))):
            yield pltpu.make_async_remote_copy(
                src_ref=src,
                dst_ref=dst.at[slot],
                send_sem=trip_send.at[kind, step],
                recv_sem=trip_recv.at[kind, step],
                device_id={"trip": peer},
                device_id_type=MESH,
            )

    def exc_copies(step, slot):
        peer = lax.rem(me_e + step, n_exc)
        for kind, (src, dst) in enumerate(((send_grid, grid_out_ref), (send_mode, mode_out_ref))):
            yield pltpu.make_async_remote_copy(
                src_ref=src.at[peer],
                dst_ref=dst.at[slot],
                send_sem=exc_send.at[kind, step],
                recv_sem=exc_recv.at[kind, step],
                device_id={"exc": peer},
                device_id_type=MESH,
            )

    for step in range(1, n_exc):
        for copy in exc_copies(step, me_e):
            copy.start()
    for step in range(1, n_trip):
        for copy in trip_copies(step, me_t):
            copy.start()
    for step in range(1, n_trip):
        for copy in trip_copies(step, lax.rem(me_t + n_trip - step, n_trip)):
            copy.wait_recv()
    for step in range(1, n_exc):
        for copy in exc_copies(step, lax.rem(me_e + n_exc - step, n_exc)):
            copy.wait_recv()
    for step in range(1, n_trip):
        for copy in trip_copies(step, me_t):
            copy.wait_send()
    for step in range(1, n_exc):
        for copy in exc_copies(step, me_e):
            copy.wait_send()


def iota(shape, axis):
    return lax.broadcasted_iota(jnp.int32, shape, axis)


def spread_by(entries, picker):
    high = entries.astype(BF16)
    rest = entries - high.astype(F32)
    mid = rest.astype(BF16)
    low = (rest - mid.astype(F32)).astype(BF16)
    dot = functools.partial(jnp.dot, preferred_element_type=F32)
    return (dot(high, picker) + dot(mid, picker)) + dot(low, picker)


PAIRS = [(a, a2) for a in range(NMOD) for a2 in range(a, NMOD)]
SLOT = {pair: index for index, pair in enumerate(PAIRS)}


def sigma_kernel(
    n_exc,
    n_blk,
    modes_ref,
    source_ref,
    live_ref,
    table_ref,
    levels_ref,
    grid_ref,
    spec_ref,
    vec_hbm,
    out_hbm,
    vec,
    out,
    mats,
    u_ref,
    left_high,
    left_low,
    picks,
    result,
    spread_ref,
    in_sem,
    out_sem,
):
    per = table_ref.shape[1]
    states = vec.shape[1]
    width = vec.shape[2]
    rows = spec_ref.shape[1]
    sub = NMOD * NMOD
    gg = G * G

    def fetch(b):
        return pltpu.make_async_copy(vec_hbm.at[b], vec.at[b], in_sem.at[b])

    def put(b):
        return pltpu.make_async_copy(out.at[b], out_hbm.at[b], out_sem.at[b])

    @pl.loop(0, n_blk)
    def _(b):
        fetch(b).start()

    key = iota((NMOD * G, gg), 0) % G
    col = iota((NMOD * G, gg), 1)
    picks[0] = jnp.where(key == col // G, 1.0, 0.0).astype(BF16)
    picks[1] = jnp.where(key == col % G, 1.0, 0.0).astype(BF16)
    per_row = width // rows
    row_pick = jnp.where(
        iota((rows, width), 0) == iota((rows, width), 1) // per_row, 1.0, 0.0
    ).astype(BF16)
    spread_ref[...] = spread_by(spec_ref[...], row_pick)[:, None, :]

    owner = iota((sub, NMOD * G), 1) // G
    row = iota((sub, NMOD * G), 0)
    is_first = owner == row // NMOD
    is_second = owner == row % NMOD
    lane = iota((sub, LANES), 1)
    lane_row = iota((sub, LANES), 0)
    lane8 = iota((sub, NMOD), 1)
    row8 = iota((sub, NMOD), 0)

    @pl.loop(0, n_exc)
    def _(p):
        def table_row(which):
            m = modes_ref[p, 0, which]
            return (
                table_ref[m // per, pl.ds(m % per, 1), :],
                levels_ref[m // per, pl.ds(m % per, 1), :],
            )

        phi_i, e_i = table_row(0)
        phi_j, e_j = table_row(1)
        phi_k, e_k = table_row(2)
        tall_j = spread_by(jnp.where(is_first, phi_j, 0.0), picks[0])
        tall_k = spread_by(jnp.where(is_second, phi_k, 0.0), picks[1])
        phi = tall_j * tall_k
        pick_i = picks[1, :, :LANES]
        pair_i = spread_by(jnp.where(is_first, phi_i, 0.0), pick_i) * spread_by(
            jnp.where(is_second, phi_i, 0.0), pick_i
        )
        u_ref[...] = jnp.dot(
            pair_i[:, :G],
            grid_ref[p],
            preferred_element_type=F32,
            precision=lax.Precision.HIGHEST,
        )
        for index, (a, a2) in enumerate(PAIRS):
            line = a * NMOD + a2
            full = phi * u_ref[line : line + 1, :]
            high = full.astype(BF16)
            left_high[index * sub : (index + 1) * sub, :] = high
            left_low[index * sub : (index + 1) * sub, :] = (full - high.astype(F32)).astype(BF16)
        phi_high = phi.astype(BF16)
        phi_low = (phi - phi_high.astype(F32)).astype(BF16)
        right = jnp.concatenate([phi_high, phi_high, phi_low, phi_low], axis=0)
        over = (((1,), (1,)), ((), ()))
        both = lax.dot_general(left_high[...], right, over, preferred_element_type=F32)
        rest = lax.dot_general(
            left_low[...], right[: 2 * sub], over, preferred_element_type=F32
        )
        result[...] = both[:, :LANES] + (both[:, LANES:] + rest)
        e_bc = jnp.sum(
            jnp.where(lane8 == row8 // NMOD, e_j, 0.0) + jnp.where(lane8 == row8 % NMOD, e_k, 0.0),
            axis=1,
            keepdims=True,
        )
        for a in range(NMOD):
            for half in range(NMOD // 2):
                even = SLOT[tuple(sorted((a, 2 * half)))]
                odd = SLOT[tuple(sorted((a, 2 * half + 1)))]
                tile = jnp.where(
                    lane < sub,
                    result[even * sub : (even + 1) * sub, :],
                    result[odd * sub : (odd + 1) * sub, :],
                )
                if a // 2 == half:
                    diagonal = e_bc + e_i[:, a : a + 1]
                    tile = tile + jnp.where(lane == lane_row + (a % 2) * sub, diagonal, 0.0)
                mats[p, a * sub : (a + 1) * sub, half * LANES : (half + 1) * LANES] = tile.astype(
                    BF16
                )

    half_width = width // 2
    half_rows = rows // 2

    @pl.loop(0, n_blk)
    def _(b):
        fetch(b).wait()
        source = source_ref[b]
        live = live_ref[b]

        def part(first):
            cols = slice(first, first + half_width)
            coeff = vec[b, :, cols]
            product = jnp.dot(mats[source], coeff, preferred_element_type=F32)
            summed = product + spread_ref[b, :, cols] * coeff.astype(F32)
            owner_row = (iota((1, half_width), 1) + first) // per_row
            out[b, :, cols] = jnp.where(owner_row < live, summed, 0.0).astype(BF16)

        part(0)

        @pl.when(live > half_rows)
        def _():
            part(half_width)

        @pl.when(live <= half_rows)
        def _():
            out[b, :, half_width:] = jnp.zeros((states, half_width), BF16)

        put(b).start()

    @pl.loop(0, n_blk)
    def _(b):
        put(b).wait()


def solution(mesh):
    n_trip, n_exc = mesh.shape["trip"], mesh.shape["exc"]
    vmem = pl.BlockSpec(memory_space=pltpu.VMEM)
    smem = pl.BlockSpec(memory_space=pltpu.SMEM)
    anywhere = pl.BlockSpec(memory_space=pl.ANY)

    def on_device(
        pes_grids,
        modals,
        energies,
        triple_modes,
        routing,
        block_source,
        live_rows,
        trial_vectors,
        spectator_energy,
    ):
        n_blk, states, width = trial_vectors.shape
        grid_shape = pes_grids.shape[1:]
        table, levels, grids, modes = pl.pallas_call(
            functools.partial(exchange, n_trip, n_exc),
            out_shape=(
                jax.ShapeDtypeStruct((n_trip,) + modals.shape, F32),
                jax.ShapeDtypeStruct((n_trip,) + energies.shape, F32),
                jax.ShapeDtypeStruct((n_exc,) + grid_shape, F32),
                jax.ShapeDtypeStruct((n_exc, 1, LANES), jnp.int32),
            ),
            in_specs=[smem, smem, vmem, vmem, vmem],
            out_specs=(vmem, vmem, vmem, vmem),
            scratch_shapes=[
                pltpu.VMEM((n_exc,) + grid_shape, F32),
                pltpu.VMEM((n_exc, 1, LANES), jnp.int32),
                pltpu.SemaphoreType.DMA((2, n_trip)),
                pltpu.SemaphoreType.DMA((2, n_trip)),
                pltpu.SemaphoreType.DMA((2, n_exc)),
                pltpu.SemaphoreType.DMA((2, n_exc)),
            ],
            compiler_params=pltpu.CompilerParams(collective_id=0, has_side_effects=True),
            name="exchange",
        )(routing, triple_modes, pes_grids, modals, energies)
        sub = NMOD * NMOD
        return pl.pallas_call(
            functools.partial(sigma_kernel, n_exc, n_blk),
            out_shape=jax.ShapeDtypeStruct(trial_vectors.shape, BF16),
            in_specs=[smem, smem, smem, vmem, vmem, vmem, vmem, anywhere],
            out_specs=anywhere,
            scratch_shapes=[
                pltpu.VMEM((n_blk, states, width), BF16),
                pltpu.VMEM((n_blk, states, width), BF16),
                pltpu.VMEM((n_exc, states, states), BF16),
                pltpu.VMEM((sub, G * G), F32),
                pltpu.VMEM((len(PAIRS) * sub, G * G), BF16),
                pltpu.VMEM((len(PAIRS) * sub, G * G), BF16),
                pltpu.VMEM((2, NMOD * G, G * G), BF16),
                pltpu.VMEM((len(PAIRS) * sub, LANES), F32),
                pltpu.VMEM((n_blk, 1, width), F32),
                pltpu.SemaphoreType.DMA((n_blk,)),
                pltpu.SemaphoreType.DMA((n_blk,)),
            ],
            compiler_params=pltpu.CompilerParams(vmem_limit_bytes=60 * 1024 * 1024),
            name="sigma",
        )(modes, block_source, live_rows, table, levels, grids, spectator_energy, trial_vectors)

    in_specs = (
        P(("trip", "exc"), None, None),
        P("trip", None),
        P("trip", None),
        P(("trip", "exc"), None),
        P("trip", None, "exc"),
        P(("trip", "exc")),
        P(("trip", "exc")),
        P(("trip", "exc"), None, None),
        P(("trip", "exc"), None),
    )
    return jax.shard_map(
        on_device,
        mesh=mesh,
        in_specs=in_specs,
        out_specs=P(("trip", "exc"), None, None),
        check_vma=False,
    )
```

```python
import functools

import jax
import jax.numpy as jnp
from jax import lax
from jax.experimental import pallas as pl
from jax.experimental.pallas import tpu as pltpu
from jax.sharding import PartitionSpec as P

NMOD = 8
G = 16
F32 = jnp.float32
BF16 = jnp.bfloat16
MESH = pl.DeviceIdType.MESH
LANES = 128


def exchange(
    n_trip,
    n_exc,
    routing_ref,
    modes_ref,
    grids_ref,
    modals_ref,
    energies_ref,
    table_ref,
    levels_ref,
    grid_out_ref,
    mode_out_ref,
    send_grid,
    send_mode,
    trip_send,
    trip_recv,
    exc_send,
    exc_recv,
):
    me_t = lax.axis_index("trip")
    me_e = lax.axis_index("exc")
    barrier = pltpu.get_barrier_semaphore()
    for step in range(1, n_exc):
        peer = lax.rem(me_e + step, n_exc)
        pl.semaphore_signal(barrier, inc=1, device_id={"exc": peer}, device_id_type=MESH)
    for step in range(1, n_trip):
        peer = lax.rem(me_t + step, n_trip)
        pl.semaphore_signal(barrier, inc=1, device_id={"trip": peer}, device_id_type=MESH)
    lane = lax.broadcasted_iota(jnp.int32, (1, LANES), 1)
    for column in range(n_exc):
        wanted = routing_ref[0, 0, column]
        send_grid[column] = grids_ref[wanted]
        send_mode[column] = jnp.where(
            lane == 0,
            modes_ref[wanted, 0],
            jnp.where(lane == 1, modes_ref[wanted, 1], modes_ref[wanted, 2]),
        )
    table_ref[me_t] = modals_ref[...]
    levels_ref[me_t] = energies_ref[...]
    grid_out_ref[me_e] = send_grid[me_e]
    mode_out_ref[me_e] = send_mode[me_e]
    pl.semaphore_wait(barrier, n_exc - 1 + n_trip - 1)

    def trip_copies(step, slot):
        peer = lax.rem(me_t + step, n_trip)
        for kind, (src, dst) in enumerate(((modals_ref, table_ref), (energies_ref, levels_ref))):
            yield pltpu.make_async_remote_copy(
                src_ref=src,
                dst_ref=dst.at[slot],
                send_sem=trip_send.at[kind, step],
                recv_sem=trip_recv.at[kind, step],
                device_id={"trip": peer},
                device_id_type=MESH,
            )

    def exc_copies(step, slot):
        peer = lax.rem(me_e + step, n_exc)
        for kind, (src, dst) in enumerate(((send_grid, grid_out_ref), (send_mode, mode_out_ref))):
            yield pltpu.make_async_remote_copy(
                src_ref=src.at[peer],
                dst_ref=dst.at[slot],
                send_sem=exc_send.at[kind, step],
                recv_sem=exc_recv.at[kind, step],
                device_id={"exc": peer},
                device_id_type=MESH,
            )

    for step in range(1, n_exc):
        for copy in exc_copies(step, me_e):
            copy.start()
    for step in range(1, n_trip):
        for copy in trip_copies(step, me_t):
            copy.start()
    for step in range(1, n_trip):
        for copy in trip_copies(step, lax.rem(me_t + n_trip - step, n_trip)):
            copy.wait_recv()
    for step in range(1, n_exc):
        for copy in exc_copies(step, lax.rem(me_e + n_exc - step, n_exc)):
            copy.wait_recv()
    for step in range(1, n_trip):
        for copy in trip_copies(step, me_t):
            copy.wait_send()
    for step in range(1, n_exc):
        for copy in exc_copies(step, me_e):
            copy.wait_send()


def iota(shape, axis):
    return lax.broadcasted_iota(jnp.int32, shape, axis)


def spread_by(entries, picker):
    high = entries.astype(BF16)
    rest = entries - high.astype(F32)
    mid = rest.astype(BF16)
    low = (rest - mid.astype(F32)).astype(BF16)
    dot = functools.partial(jnp.dot, preferred_element_type=F32)
    return (dot(high, picker) + dot(mid, picker)) + dot(low, picker)


PAIRS = [(a, a2) for a in range(NMOD) for a2 in range(a, NMOD)]
SLOT = {pair: index for index, pair in enumerate(PAIRS)}


def sigma_kernel(
    n_exc,
    n_blk,
    modes_ref,
    source_ref,
    live_ref,
    table_ref,
    levels_ref,
    grid_ref,
    spec_ref,
    vec_hbm,
    out_hbm,
    vec,
    out,
    mats,
    u_ref,
    left_high,
    left_low,
    picks,
    result,
    spread_ref,
    in_sem,
    out_sem,
):
    per = table_ref.shape[1]
    states = vec.shape[1]
    width = vec.shape[2]
    rows = spec_ref.shape[0]
    sub = NMOD * NMOD
    gg = G * G

    def fetch(b):
        return pltpu.make_async_copy(vec_hbm.at[b], vec.at[b], in_sem.at[b])

    def put(b):
        return pltpu.make_async_copy(out.at[b], out_hbm.at[b], out_sem.at[b])

    @pl.loop(0, n_blk)
    def _(b):
        fetch(b).start()

    key = iota((NMOD * G, gg), 0) % G
    col = iota((NMOD * G, gg), 1)
    picks[0] = jnp.where(key == col // G, 1.0, 0.0).astype(BF16)
    picks[1] = jnp.where(key == col % G, 1.0, 0.0).astype(BF16)
    per_row = width // rows
    row_pick = jnp.where(
        iota((rows, width), 0) == iota((rows, width), 1) // per_row, 1.0, 0.0
    ).astype(BF16)
    spread_ref[...] = spread_by(spec_ref[...].T, row_pick)[:, None, :]

    owner = iota((sub, NMOD * G), 1) // G
    row = iota((sub, NMOD * G), 0)
    is_first = owner == row // NMOD
    is_second = owner == row % NMOD
    lane = iota((sub, LANES), 1)
    lane_row = iota((sub, LANES), 0)

    @pl.loop(0, n_exc)
    def _(p):
        def table_row(which):
            m = modes_ref[p, 0, which]
            tile = levels_ref[m // per]
            here = iota(tile.shape, 1) == m % per
            return (
                table_ref[m // per, pl.ds(m % per, 1), :],
                jnp.sum(jnp.where(here, tile, 0.0), axis=1, keepdims=True),
            )

        phi_i, e_i = table_row(0)
        phi_j, e_j = table_row(1)
        phi_k, e_k = table_row(2)
        tall_j = spread_by(jnp.where(is_first, phi_j, 0.0), picks[0])
        tall_k = spread_by(jnp.where(is_second, phi_k, 0.0), picks[1])
        phi = tall_j * tall_k
        pick_i = picks[1, :, :LANES]
        pair_i = spread_by(jnp.where(is_first, phi_i, 0.0), pick_i) * spread_by(
            jnp.where(is_second, phi_i, 0.0), pick_i
        )
        u_ref[...] = jnp.dot(
            pair_i[:, :G],
            grid_ref[p],
            preferred_element_type=F32,
            precision=lax.Precision.HIGHEST,
        )
        for index, (a, a2) in enumerate(PAIRS):
            line = a * NMOD + a2
            full = phi * u_ref[line : line + 1, :]
            high = full.astype(BF16)
            left_high[index * sub : (index + 1) * sub, :] = high
            left_low[index * sub : (index + 1) * sub, :] = (full - high.astype(F32)).astype(BF16)
        phi_high = phi.astype(BF16)
        phi_low = (phi - phi_high.astype(F32)).astype(BF16)
        right = jnp.concatenate([phi_high, phi_high, phi_low, phi_low], axis=0)
        over = (((1,), (1,)), ((), ()))
        both = lax.dot_general(left_high[...], right, over, preferred_element_type=F32)
        rest = lax.dot_general(
            left_low[...], right[: 2 * sub], over, preferred_element_type=F32
        )
        result[...] = both[:, :LANES] + (both[:, LANES:] + rest)
        e_bc = jnp.concatenate([e_j[b : b + 1, :] + e_k for b in range(NMOD)], axis=0)
        for a in range(NMOD):
            for half in range(NMOD // 2):
                even = SLOT[tuple(sorted((a, 2 * half)))]
                odd = SLOT[tuple(sorted((a, 2 * half + 1)))]
                tile = jnp.where(
                    lane < sub,
                    result[even * sub : (even + 1) * sub, :],
                    result[odd * sub : (odd + 1) * sub, :],
                )
                if a // 2 == half:
                    diagonal = e_bc + e_i[a : a + 1, :]
                    tile = tile + jnp.where(lane == lane_row + (a % 2) * sub, diagonal, 0.0)
                mats[p, a * sub : (a + 1) * sub, half * LANES : (half + 1) * LANES] = tile.astype(
                    BF16
                )

    half_width = width // 2
    half_rows = rows // 2

    @pl.loop(0, n_blk)
    def _(b):
        fetch(b).wait()
        source = source_ref[b]
        live = live_ref[b]

        def part(first):
            cols = slice(first, first + half_width)
            coeff = vec[b, :, cols]
            product = jnp.dot(mats[source], coeff, preferred_element_type=F32)
            summed = product + spread_ref[b, :, cols] * coeff.astype(F32)
            owner_row = (iota((1, half_width), 1) + first) // per_row
            out[b, :, cols] = jnp.where(owner_row < live, summed, 0.0).astype(BF16)

        part(0)

        @pl.when(live > half_rows)
        def _():
            part(half_width)

        @pl.when(live <= half_rows)
        def _():
            out[b, :, half_width:] = jnp.zeros((states, half_width), BF16)

        put(b).start()

    @pl.loop(0, n_blk)
    def _(b):
        put(b).wait()


def solution(mesh):
    n_trip, n_exc = mesh.shape["trip"], mesh.shape["exc"]
    vmem = pl.BlockSpec(memory_space=pltpu.VMEM)
    smem = pl.BlockSpec(memory_space=pltpu.SMEM)
    anywhere = pl.BlockSpec(memory_space=pl.ANY)

    def on_device(
        pes_grids,
        modals,
        energies,
        triple_modes,
        routing,
        block_source,
        live_rows,
        trial_vectors,
        spectator_energy,
    ):
        n_blk, states, width = trial_vectors.shape
        grid_shape = pes_grids.shape[1:]
        table, levels, grids, modes = pl.pallas_call(
            functools.partial(exchange, n_trip, n_exc),
            out_shape=(
                jax.ShapeDtypeStruct((n_trip,) + modals.shape, F32),
                jax.ShapeDtypeStruct((n_trip,) + energies.T.shape, F32),
                jax.ShapeDtypeStruct((n_exc,) + grid_shape, F32),
                jax.ShapeDtypeStruct((n_exc, 1, LANES), jnp.int32),
            ),
            in_specs=[smem, smem, vmem, vmem, vmem],
            out_specs=(vmem, vmem, vmem, vmem),
            scratch_shapes=[
                pltpu.VMEM((n_exc,) + grid_shape, F32),
                pltpu.VMEM((n_exc, 1, LANES), jnp.int32),
                pltpu.SemaphoreType.DMA((2, n_trip)),
                pltpu.SemaphoreType.DMA((2, n_trip)),
                pltpu.SemaphoreType.DMA((2, n_exc)),
                pltpu.SemaphoreType.DMA((2, n_exc)),
            ],
            compiler_params=pltpu.CompilerParams(collective_id=0, has_side_effects=True),
            name="exchange",
        )(jnp.swapaxes(routing, 1, 2), triple_modes, pes_grids, modals, energies.T)
        sub = NMOD * NMOD
        return pl.pallas_call(
            functools.partial(sigma_kernel, n_exc, n_blk),
            out_shape=jax.ShapeDtypeStruct(trial_vectors.shape, BF16),
            in_specs=[smem, smem, smem, vmem, vmem, vmem, vmem, anywhere],
            out_specs=anywhere,
            scratch_shapes=[
                pltpu.VMEM((n_blk, states, width), BF16),
                pltpu.VMEM((n_blk, states, width), BF16),
                pltpu.VMEM((n_exc, states, states), BF16),
                pltpu.VMEM((sub, G * G), F32),
                pltpu.VMEM((len(PAIRS) * sub, G * G), BF16),
                pltpu.VMEM((len(PAIRS) * sub, G * G), BF16),
                pltpu.VMEM((2, NMOD * G, G * G), BF16),
                pltpu.VMEM((len(PAIRS) * sub, LANES), F32),
                pltpu.VMEM((n_blk, 1, width), F32),
                pltpu.SemaphoreType.DMA((n_blk,)),
                pltpu.SemaphoreType.DMA((n_blk,)),
            ],
            compiler_params=pltpu.CompilerParams(vmem_limit_bytes=60 * 1024 * 1024),
            name="sigma",
        )(modes, block_source, live_rows, table, levels, grids, spectator_energy.T, trial_vectors)

    in_specs = (
        P(("trip", "exc"), None, None),
        P("trip", None),
        P("trip", None),
        P(("trip", "exc"), None),
        P("trip", None, "exc"),
        P(("trip", "exc")),
        P(("trip", "exc")),
        P(("trip", "exc"), None, None),
        P(("trip", "exc"), None),
    )
    return jax.shard_map(
        on_device,
        mesh=mesh,
        in_specs=in_specs,
        out_specs=P(("trip", "exc"), None, None),
        check_vma=False,
    )
```

```python
import functools

import jax
import jax.numpy as jnp
from jax import lax
from jax.experimental import pallas as pl
from jax.experimental.pallas import tpu as pltpu
from jax.sharding import PartitionSpec as P

NMOD = 8
G = 16
F32 = jnp.float32
BF16 = jnp.bfloat16
MESH = pl.DeviceIdType.MESH
LANES = 128


def exchange(
    n_trip,
    n_exc,
    routing_ref,
    modes_ref,
    grids_ref,
    modals_ref,
    energies_ref,
    table_ref,
    levels_ref,
    grid_out_ref,
    mode_out_ref,
    send_grid,
    send_mode,
    trip_send,
    trip_recv,
    exc_send,
    exc_recv,
):
    me_t = lax.axis_index("trip")
    me_e = lax.axis_index("exc")
    barrier = pltpu.get_barrier_semaphore()
    for step in range(1, n_exc):
        peer = lax.rem(me_e + step, n_exc)
        pl.semaphore_signal(barrier, inc=1, device_id={"exc": peer}, device_id_type=MESH)
    for step in range(1, n_trip):
        peer = lax.rem(me_t + step, n_trip)
        pl.semaphore_signal(barrier, inc=1, device_id={"trip": peer}, device_id_type=MESH)
    lane = lax.broadcasted_iota(jnp.int32, (1, LANES), 1)
    for column in range(n_exc):
        wanted = routing_ref[0, 0, column]
        send_grid[column] = grids_ref[wanted]
        send_mode[column] = jnp.where(
            lane == 0,
            modes_ref[wanted, 0],
            jnp.where(lane == 1, modes_ref[wanted, 1], modes_ref[wanted, 2]),
        )
    table_ref[me_t] = modals_ref[...]
    levels_ref[me_t] = energies_ref[...]
    grid_out_ref[me_e] = send_grid[me_e]
    mode_out_ref[me_e] = send_mode[me_e]
    pl.semaphore_wait(barrier, n_exc - 1 + n_trip - 1)

    def trip_copies(step, slot):
        peer = lax.rem(me_t + step, n_trip)
        for kind, (src, dst) in enumerate(((modals_ref, table_ref), (energies_ref, levels_ref))):
            yield pltpu.make_async_remote_copy(
                src_ref=src,
                dst_ref=dst.at[slot],
                send_sem=trip_send.at[kind, step],
                recv_sem=trip_recv.at[kind, step],
                device_id={"trip": peer},
                device_id_type=MESH,
            )

    def exc_copies(step, slot):
        peer = lax.rem(me_e + step, n_exc)
        for kind, (src, dst) in enumerate(((send_grid, grid_out_ref), (send_mode, mode_out_ref))):
            yield pltpu.make_async_remote_copy(
                src_ref=src.at[peer],
                dst_ref=dst.at[slot],
                send_sem=exc_send.at[kind, step],
                recv_sem=exc_recv.at[kind, step],
                device_id={"exc": peer},
                device_id_type=MESH,
            )

    for step in range(1, n_exc):
        for copy in exc_copies(step, me_e):
            copy.start()
    for step in range(1, n_trip):
        for copy in trip_copies(step, me_t):
            copy.start()
    for step in range(1, n_trip):
        for copy in trip_copies(step, lax.rem(me_t + n_trip - step, n_trip)):
            copy.wait_recv()
    for step in range(1, n_exc):
        for copy in exc_copies(step, lax.rem(me_e + n_exc - step, n_exc)):
            copy.wait_recv()
    for step in range(1, n_trip):
        for copy in trip_copies(step, me_t):
            copy.wait_send()
    for step in range(1, n_exc):
        for copy in exc_copies(step, me_e):
            copy.wait_send()


def iota(shape, axis):
    return lax.broadcasted_iota(jnp.int32, shape, axis)


def spread_by(entries, picker):
    high = entries.astype(BF16)
    rest = entries - high.astype(F32)
    mid = rest.astype(BF16)
    low = (rest - mid.astype(F32)).astype(BF16)
    dot = functools.partial(jnp.dot, preferred_element_type=F32)
    return (dot(high, picker) + dot(mid, picker)) + dot(low, picker)


PAIRS = [(a, a2) for a in range(NMOD) for a2 in range(a, NMOD)]
SLOT = {pair: index for index, pair in enumerate(PAIRS)}


def sigma_kernel(
    n_exc,
    n_blk,
    modes_ref,
    source_ref,
    live_ref,
    table_ref,
    levels_ref,
    grid_ref,
    spec_ref,
    vec_hbm,
    out_hbm,
    vec,
    out,
    mats,
    u_ref,
    left_high,
    picks,
    result,
    spread_ref,
    in_sem,
    out_sem,
):
    per = table_ref.shape[1]
    states = vec.shape[1]
    width = vec.shape[2]
    rows = spec_ref.shape[0]
    sub = NMOD * NMOD
    gg = G * G

    def fetch(b):
        return pltpu.make_async_copy(vec_hbm.at[b], vec.at[b], in_sem.at[b])

    def put(b):
        return pltpu.make_async_copy(out.at[b], out_hbm.at[b], out_sem.at[b])

    @pl.loop(0, n_blk)
    def _(b):
        fetch(b).start()

    key = iota((NMOD * G, gg), 0) % G
    col = iota((NMOD * G, gg), 1)
    picks[0] = jnp.where(key == col // G, 1.0, 0.0).astype(BF16)
    picks[1] = jnp.where(key == col % G, 1.0, 0.0).astype(BF16)
    per_row = width // rows
    row_pick = jnp.where(
        iota((rows, width), 0) == iota((rows, width), 1) // per_row, 1.0, 0.0
    ).astype(BF16)
    spread_ref[...] = spread_by(spec_ref[...].T, row_pick)[:, None, :]

    owner = iota((sub, NMOD * G), 1) // G
    row = iota((sub, NMOD * G), 0)
    is_first = owner == row // NMOD
    is_second = owner == row % NMOD
    lane = iota((sub, LANES), 1)
    lane_row = iota((sub, LANES), 0)

    @pl.loop(0, n_exc)
    def _(p):
        def table_row(which):
            m = modes_ref[p, 0, which]
            tile = levels_ref[m // per]
            here = iota(tile.shape, 1) == m % per
            return (
                table_ref[m // per, pl.ds(m % per, 1), :],
                jnp.sum(jnp.where(here, tile, 0.0), axis=1, keepdims=True),
            )

        phi_i, e_i = table_row(0)
        phi_j, e_j = table_row(1)
        phi_k, e_k = table_row(2)
        tall_j = spread_by(jnp.where(is_first, phi_j, 0.0), picks[0])
        tall_k = spread_by(jnp.where(is_second, phi_k, 0.0), picks[1])
        phi = tall_j * tall_k
        pick_i = picks[1, :, :LANES]
        pair_i = spread_by(jnp.where(is_first, phi_i, 0.0), pick_i) * spread_by(
            jnp.where(is_second, phi_i, 0.0), pick_i
        )
        u_ref[...] = jnp.dot(
            pair_i[:, :G],
            grid_ref[p],
            preferred_element_type=F32,
            precision=lax.Precision.HIGHEST,
        )
        for index, (a, a2) in enumerate(PAIRS):
            line = a * NMOD + a2
            full = phi * u_ref[line : line + 1, :]
            left_high[index * sub : (index + 1) * sub, :] = full.astype(BF16)
        phi_high = phi.astype(BF16)
        phi_low = (phi - phi_high.astype(F32)).astype(BF16)
        right = jnp.concatenate([phi_high, phi_high, phi_low, phi_low], axis=0)
        over = (((1,), (1,)), ((), ()))
        both = lax.dot_general(left_high[...], right, over, preferred_element_type=F32)
        result[...] = both[:, :LANES] + both[:, LANES:]
        e_bc = jnp.concatenate([e_j[b : b + 1, :] + e_k for b in range(NMOD)], axis=0)
        for a in range(NMOD):
            for half in range(NMOD // 2):
                even = SLOT[tuple(sorted((a, 2 * half)))]
                odd = SLOT[tuple(sorted((a, 2 * half + 1)))]
                tile = jnp.where(
                    lane < sub,
                    result[even * sub : (even + 1) * sub, :],
                    result[odd * sub : (odd + 1) * sub, :],
                )
                if a // 2 == half:
                    diagonal = e_bc + e_i[a : a + 1, :]
                    tile = tile + jnp.where(lane == lane_row + (a % 2) * sub, diagonal, 0.0)
                mats[p, a * sub : (a + 1) * sub, half * LANES : (half + 1) * LANES] = tile.astype(
                    BF16
                )

    half_width = width // 2
    half_rows = rows // 2

    @pl.loop(0, n_blk)
    def _(b):
        fetch(b).wait()
        source = source_ref[b]
        live = live_ref[b]

        def part(first):
            cols = slice(first, first + half_width)
            coeff = vec[b, :, cols]
            product = jnp.dot(mats[source], coeff, preferred_element_type=F32)
            summed = product + spread_ref[b, :, cols] * coeff.astype(F32)
            owner_row = (iota((1, half_width), 1) + first) // per_row
            out[b, :, cols] = jnp.where(owner_row < live, summed, 0.0).astype(BF16)

        part(0)

        @pl.when(live > half_rows)
        def _():
            part(half_width)

        @pl.when(live <= half_rows)
        def _():
            out[b, :, half_width:] = jnp.zeros((states, half_width), BF16)

        put(b).start()

    @pl.loop(0, n_blk)
    def _(b):
        put(b).wait()


def solution(mesh):
    n_trip, n_exc = mesh.shape["trip"], mesh.shape["exc"]
    vmem = pl.BlockSpec(memory_space=pltpu.VMEM)
    smem = pl.BlockSpec(memory_space=pltpu.SMEM)
    anywhere = pl.BlockSpec(memory_space=pl.ANY)

    def on_device(
        pes_grids,
        modals,
        energies,
        triple_modes,
        routing,
        block_source,
        live_rows,
        trial_vectors,
        spectator_energy,
    ):
        n_blk, states, width = trial_vectors.shape
        grid_shape = pes_grids.shape[1:]
        table, levels, grids, modes = pl.pallas_call(
            functools.partial(exchange, n_trip, n_exc),
            out_shape=(
                jax.ShapeDtypeStruct((n_trip,) + modals.shape, F32),
                jax.ShapeDtypeStruct((n_trip,) + energies.T.shape, F32),
                jax.ShapeDtypeStruct((n_exc,) + grid_shape, F32),
                jax.ShapeDtypeStruct((n_exc, 1, LANES), jnp.int32),
            ),
            in_specs=[smem, smem, vmem, vmem, vmem],
            out_specs=(vmem, vmem, vmem, vmem),
            scratch_shapes=[
                pltpu.VMEM((n_exc,) + grid_shape, F32),
                pltpu.VMEM((n_exc, 1, LANES), jnp.int32),
                pltpu.SemaphoreType.DMA((2, n_trip)),
                pltpu.SemaphoreType.DMA((2, n_trip)),
                pltpu.SemaphoreType.DMA((2, n_exc)),
                pltpu.SemaphoreType.DMA((2, n_exc)),
            ],
            compiler_params=pltpu.CompilerParams(collective_id=0, has_side_effects=True),
            name="exchange",
        )(jnp.swapaxes(routing, 1, 2), triple_modes, pes_grids, modals, energies.T)
        sub = NMOD * NMOD
        return pl.pallas_call(
            functools.partial(sigma_kernel, n_exc, n_blk),
            out_shape=jax.ShapeDtypeStruct(trial_vectors.shape, BF16),
            in_specs=[smem, smem, smem, vmem, vmem, vmem, vmem, anywhere],
            out_specs=anywhere,
            scratch_shapes=[
                pltpu.VMEM((n_blk, states, width), BF16),
                pltpu.VMEM((n_blk, states, width), BF16),
                pltpu.VMEM((n_exc, states, states), BF16),
                pltpu.VMEM((sub, G * G), F32),
                pltpu.VMEM((len(PAIRS) * sub, G * G), BF16),
                pltpu.VMEM((2, NMOD * G, G * G), BF16),
                pltpu.VMEM((len(PAIRS) * sub, LANES), F32),
                pltpu.VMEM((n_blk, 1, width), F32),
                pltpu.SemaphoreType.DMA((n_blk,)),
                pltpu.SemaphoreType.DMA((n_blk,)),
            ],
            compiler_params=pltpu.CompilerParams(vmem_limit_bytes=60 * 1024 * 1024),
            name="sigma",
        )(modes, block_source, live_rows, table, levels, grids, spectator_energy.T, trial_vectors)

    in_specs = (
        P(("trip", "exc"), None, None),
        P("trip", None),
        P("trip", None),
        P(("trip", "exc"), None),
        P("trip", None, "exc"),
        P(("trip", "exc")),
        P(("trip", "exc")),
        P(("trip", "exc"), None, None),
        P(("trip", "exc"), None),
    )
    return jax.shard_map(
        on_device,
        mesh=mesh,
        in_specs=in_specs,
        out_specs=P(("trip", "exc"), None, None),
        check_vma=False,
    )
```
